256 devices in a mesh: seq: 32 (over x, y, core), dp: 8 (over z).
Axes of the slice: x: 4, y: 4, z: 8, core: 2. Of those that a mesh axis runs over, the one named last changes fastest.
Arguments:
- points: bfloat16 [8, 16384, 512], P('dp', 'seq'), may hold values from -6 to 6
- cotangent: bfloat16 [8, 16384, 512], P('dp', 'seq'), may hold values from -6 to 6
- dest: int32 [8, 16384], P('dp', 'seq'), may hold values from 0 to 16383, as said below
- w_qkv: bfloat16 [512, 1536], replicated
- w_proj: bfloat16 [512, 512], replicated, may hold values from -0.25 to 0.25
- gain: float32 [512], replicated, may hold values from 0.5 to 1.5
Outputs:
- grad_points: bfloat16 [8, 16384, 512], P('dp', 'seq')
- grad_qkv: float32 [512, 1536], replicated
- grad_proj: float32 [512, 512], replicated
- gain_gradient: float32 [512], replicated
The draws below stay inside these ranges and needn't reach their ends.
Inputs may be any that keep to these rules, and one draw needn't show every extreme that they name: For each scan, dest is a permutation of the 16384 positions, one serialization order of the points. Of the 512 points of one device, at most 32 have positions on any one device's range of 512 positions, and exactly 32 for some device.
All inputs are finite; a program needn't handle non-finite values.
Results may differ from the reference program's by a relative error of at most 0.013.
The reference program's roundings to bfloat16 on the way count: a program that leaves them out, or rounds other values in their place, can miss the bound.
Values may be sent and summed in bfloat16 or wider, within the bound.
A program may use at most 64 MiB of HBM per device.

```python
import jax
import jax.numpy as jnp
from jax import lax

C = 512
HEADS = 8
HD = 64
PATCH = 512
P_DEV = 512
N_PTS = 16384
SCANS = 8
N_SEQ = 32


def draw_dest(key, part):

    def one_scan(scan_key):
        unit = P_DEV // N_SEQ
        key_gain, key_loss, key_source, key_target = jax.random.split(scan_key, 4)
        shift_gain = jax.random.randint(key_gain, (), 0, N_SEQ)
        shift_loss = (shift_gain + jax.random.randint(key_loss, (), 1, N_SEQ)) % N_SEQ
        device = jnp.arange(N_SEQ, dtype=jnp.int32)[:, None]
        local = jnp.arange(P_DEV, dtype=jnp.int32)[None, :]
        block = local // unit
        offset = local % unit
        moved = block == (device + shift_loss) % N_SEQ
        target = jnp.where(moved, (device + shift_gain) % N_SEQ, block)
        slot = jnp.where(moved, (device + shift_gain - shift_loss) % N_SEQ * unit + offset, device * unit + offset)
        orders = jax.vmap(lambda sub: jax.random.permutation(sub, P_DEV))(jax.random.split(key_target, N_SEQ))
        within = orders[target, slot]
        position = target * P_DEV + within
        mixing = jax.vmap(lambda sub: jax.random.permutation(sub, P_DEV))(jax.random.split(key_source, N_SEQ))
        device_full = jnp.broadcast_to(device, (N_SEQ, P_DEV))
        placed = jnp.zeros((N_SEQ, P_DEV), jnp.int32).at[device_full, mixing].set(position.astype(jnp.int32))
        return placed.reshape(-1)
    return jax.vmap(one_scan)(jax.random.split(key, SCANS))


def draw_w_qkv(key, part):
    base = jax.random.normal(key, (C, 3 * C), jnp.float32) * C ** (-0.5)
    return base.astype(jnp.bfloat16)


def block_levels(rng, dims, cuts, smallest, high):
    def one(dim, blocks):
        heights = jax.random.uniform(jax.random.fold_in(jax.random.fold_in(rng, 6), dim), (blocks,), jnp.float32, smallest / len(cuts), high / len(cuts))
        return jnp.repeat(jnp.exp(heights), dims[dim] // blocks).reshape((-1,) + (1,) * (len(dims) - dim - 1))

    level = one(*cuts[0])
    for cut in cuts[1:]:
        level = level * one(*cut)
    return level


def noise(rng, extent, deviation, limit, cuts=(), kind=jnp.bfloat16):
    array = jax.random.normal(rng, extent, jnp.float32) * deviation
    if len(cuts) > 0:
        array = block_levels(rng, extent, cuts, -0.22, 0.18) * array
    return jnp.clip(array, min=-limit, max=limit).astype(kind)


def setup_inputs(seed: int = 0) -> dict:
    key_list = jax.random.split(jax.random.key(seed), 7)
    points = noise(key_list[0], (SCANS, N_PTS, C), 1.0, 6.0, ((0, 8), (1, 32)))
    cotangent = noise(key_list[1], (SCANS, N_PTS, C), 1.0, 6.0, ((0, 8), (1, 32)))
    dest = draw_dest(jax.random.fold_in(key_list[6], 71), 0)
    w_qkv = draw_w_qkv(jax.random.fold_in(key_list[6], 71), 0)
    w_proj = noise(key_list[4], (C, C), C ** -0.5, 0.25)
    gain = jnp.clip(1.0 + 0.1 * jax.random.normal(key_list[5], (C,), jnp.float32), 0.5, 1.5)
    return dict(points=points, cotangent=cotangent, dest=dest, w_qkv=w_qkv, w_proj=w_proj, gain=gain)


def block_backward(serial, serial_grad, w_qkv, w_proj, gain):
    rows_all = serial.shape[0]
    feats = serial.astype(jnp.float32)
    centered_input = feats - lax.optimization_barrier(jnp.mean(feats, axis=1, keepdims=True))
    inverse_deviation = lax.rsqrt(lax.optimization_barrier(jnp.mean(centered_input * centered_input, axis=1, keepdims=True)) + 1e-05)
    standardized_input = centered_input * inverse_deviation
    normalized_input = (standardized_input * gain[None, :]).astype(jnp.bfloat16)
    qkv = jnp.dot(normalized_input, w_qkv, preferred_element_type=jnp.float32).astype(jnp.bfloat16)
    d_attn = jnp.dot(serial_grad, w_proj.T, preferred_element_type=jnp.float32).astype(jnp.bfloat16)
    patches = rows_all // PATCH
    scale = 1.0 / HD ** 0.5
    attn_list, dq_list, dk_list, dv_list = ([], [], [], [])
    for head_idx in range(HEADS):
        lo_col = head_idx * HD
        query = qkv[:, lo_col:lo_col + HD].reshape(patches, PATCH, HD).astype(jnp.float32)
        keys = qkv[:, C + lo_col:C + lo_col + HD].reshape(patches, PATCH, HD).astype(jnp.float32)
        values = qkv[:, 2 * C + lo_col:2 * C + lo_col + HD].reshape(patches, PATCH, HD).astype(jnp.float32)
        grad_head = d_attn[:, lo_col:lo_col + HD].reshape(patches, PATCH, HD).astype(jnp.float32)
        scores = jnp.einsum('pqd,pkd->pqk', query, keys) * scale
        top = lax.optimization_barrier(jnp.max(scores, axis=2, keepdims=True))
        expo = jnp.exp(scores - top)
        probs = expo / lax.optimization_barrier(jnp.sum(expo, axis=2, keepdims=True))
        probs_b = probs.astype(jnp.bfloat16).astype(jnp.float32)
        attn_list.append(jnp.einsum('pqk,pkd->pqd', probs_b, values).astype(jnp.bfloat16).reshape(rows_all, HD))
        d_probs = jnp.einsum('pqd,pkd->pqk', grad_head, values)
        d_scores = probs * (d_probs - lax.optimization_barrier(jnp.sum(d_probs * probs, axis=2, keepdims=True))) * scale
        d_scores = d_scores.astype(jnp.bfloat16).astype(jnp.float32)
        dq_list.append(jnp.einsum('pqk,pkd->pqd', d_scores, keys).astype(jnp.bfloat16).reshape(rows_all, HD))
        dk_list.append(jnp.einsum('pqk,pqd->pkd', d_scores, query).astype(jnp.bfloat16).reshape(rows_all, HD))
        dv_list.append(jnp.einsum('pqk,pqd->pkd', probs_b, grad_head).astype(jnp.bfloat16).reshape(rows_all, HD))
    attn = jnp.concatenate(attn_list, axis=1)
    d_qkv = jnp.concatenate(dq_list + dk_list + dv_list, axis=1)
    grad_proj = jnp.dot(attn.T, serial_grad, preferred_element_type=jnp.float32)
    grad_qkv = jnp.dot(normalized_input.T, d_qkv, preferred_element_type=jnp.float32)
    normalized_gradient = jnp.dot(d_qkv, w_qkv.T, preferred_element_type=jnp.float32)
    gain_gradient = lax.optimization_barrier(jnp.sum(normalized_gradient * standardized_input, axis=0))
    gain_scaled = normalized_gradient * gain[None, :]
    residual_branch = inverse_deviation * (gain_scaled - lax.optimization_barrier(jnp.mean(gain_scaled, axis=1, keepdims=True)) - standardized_input * lax.optimization_barrier(jnp.mean(gain_scaled * standardized_input, axis=1, keepdims=True)))
    serial_dx = (serial_grad.astype(jnp.float32) + residual_branch).astype(jnp.bfloat16)
    return (serial_dx, grad_qkv, grad_proj, gain_gradient)

def reference(points, cotangent, dest, w_qkv, w_proj, gain):

    def one_scan(operands):
        feats, grads, places = operands
        serial = jnp.zeros_like(feats).at[places].set(feats)
        serial_grad = jnp.zeros_like(grads).at[places].set(grads)
        serial_dx, grad_qkv, grad_proj, gain_gradient = block_backward(serial, serial_grad, w_qkv, w_proj, gain)
        return (serial_dx[places], grad_qkv, grad_proj, gain_gradient)
    grad_points, grad_qkv, grad_proj, gain_gradient = lax.map(one_scan, (points, cotangent, dest))
    return (grad_points, lax.optimization_barrier(jnp.sum(grad_qkv, axis=0)), lax.optimization_barrier(jnp.sum(grad_proj, axis=0)), lax.optimization_barrier(jnp.sum(gain_gradient, axis=0)))
```

```python
import jax
import jax.numpy as jnp
from jax import lax
from jax.experimental import pallas as pl
from jax.experimental.pallas import tpu as pltpu
from jax.sharding import Mesh
from jax.sharding import PartitionSpec as P

SEQ = ("seq_0", "seq_1", "seq_2")
MESH_ID = pl.DeviceIdType.MESH
F32, BF16 = jnp.float32, jnp.bfloat16
ROWS = 512
C = 512
N_SEQ = 32
CAP = 32
SLOTS = N_SEQ * CAP
HEADS, HD = 8, 64
PAIRS = HEADS // 2
SCALE = 1.0 / HD**0.5
CHUNK = 2048


def nn(a, b):
    return jnp.dot(a, b, preferred_element_type=F32)


def nt(a, b):
    return lax.dot_general(a, b, (((1,), (1,)), ((), ())), preferred_element_type=F32)


def iota(shape, dim):
    return lax.broadcasted_iota(jnp.int32, shape, dim)


def hot(cond):
    return jnp.where(cond, 1.0, 0.0).astype(BF16)


def remote(src, dst, send, recv, device):
    return pltpu.make_async_remote_copy(
        src_ref=src, dst_ref=dst, send_sem=send, recv_sem=recv, device_id=device, device_id_type=MESH_ID
    )


def seq_peer(mx, my, mc, d, sign):
    dx, dy, dc = d // 8, (d // 2) % 4, d % 2
    return {
        "seq_0": lax.rem(mx + (dx if sign > 0 else 4 - dx), 4),
        "seq_1": lax.rem(my + (dy if sign > 0 else 4 - dy), 4),
        "seq_2": lax.rem(mc + dc, 2),
    }


def block_kernel(
    dest_ref, pts_ref, cot_ref, wqkv_ref, wproj_ref, gain_ref,
    out_ref, grads_ref, gg_ref,
    send_a, recv_a, send_b, recv_b, back, pos_send, pos_recv, pos_all,
    qkv, dattn, sgrad, xhat, invs, normed_t, dqkv, attn_t, probs, onehot_u, onehot_ut, onehot_pt,
    sem_send, sem_recv,
):
    mx, my, mc = lax.axis_index("seq_0"), lax.axis_index("seq_1"), lax.axis_index("seq_2")
    here = {"seq_0": mx, "seq_1": my, "seq_2": mc}
    barrier = pltpu.get_barrier_semaphore()
    for d in range(1, N_SEQ):
        pl.semaphore_signal(barrier, inc=1, device_id=seq_peer(mx, my, mc, d, 1), device_id_type=MESH_ID)

    dest = dest_ref[...]
    owner, slot = dest >> 9, dest & 511
    rel = ((((owner >> 3) - mx) & 3) << 3) | ((((owner >> 1) - my) & 3) << 1) | ((owner - mc) & 1)
    to_hot_f = jnp.where(iota((N_SEQ, ROWS), 0) == rel, 1.0, 0.0)
    to_hot = to_hot_f.astype(BF16)
    earlier = hot(iota((ROWS, ROWS), 0) < iota((ROWS, ROWS), 1))
    rank = jnp.sum(to_hot_f * nn(to_hot, earlier), axis=0, keepdims=True).astype(jnp.int32)
    sid = rel * CAP + rank
    rank_hot = hot(iota((128, ROWS), 0) == rank)
    pos_hi = nt((to_hot_f * (slot >> 4).astype(F32)).astype(BF16), rank_hot)
    pos_lo = nt((to_hot_f * (slot & 15).astype(F32)).astype(BF16), rank_hot)
    pos = pos_hi * 16.0 + pos_lo
    for d in range(N_SEQ):
        pos_send[d] = pos[d : d + 1, :]

    def pack(src_ref, send_ref, recv_ref):
        data = src_ref[...]

        def step(b, _):
            rows = pl.ds(pl.multiple_of(b * 256, 256), 256)
            pick = hot(iota((256, ROWS), 0) + b * 256 == sid)
            send_ref[rows, :] = nn(pick, data).astype(BF16)
            return 0

        lax.fori_loop(0, SLOTS // 256, step, 0)
        recv_ref[0:CAP, :] = send_ref[0:CAP, :]

    def send_all(send_ref, recv_ref, index, sign):
        for d in range(1, N_SEQ):
            rows = pl.ds(d * CAP, CAP)
            remote(send_ref.at[rows], recv_ref.at[rows], sem_send.at[index], sem_recv.at[index],
                   seq_peer(mx, my, mc, d, sign)).start()

    def wait_recv(ref, index):
        remote(ref, ref, sem_send.at[index], sem_recv.at[index], here).wait_recv()

    def wait_send(ref, index):
        remote(ref, ref, sem_send.at[index], sem_recv.at[index], here).wait_send()

    pack(pts_ref, send_a, recv_a)
    pl.semaphore_wait(barrier, N_SEQ - 1)
    for d in range(1, N_SEQ):
        remote(pos_send.at[d], pos_recv.at[d], sem_send.at[2], sem_recv.at[2],
               seq_peer(mx, my, mc, d, 1)).start()
    send_all(send_a, recv_a, 0, 1)
    pack(cot_ref, send_b, recv_b)
    send_all(send_b, recv_b, 1, 1)

    sid_col = jnp.transpose(jnp.broadcast_to(sid.astype(F32), (128, ROWS))).astype(jnp.int32)
    for j in range(SLOTS // 128):
        onehot_pt[:, j * 128 : (j + 1) * 128] = hot(iota((ROWS, 128), 1) + j * 128 == sid_col)

    others = pl.ds(CAP, SLOTS - CAP)
    wait_recv(pos_recv.at[pl.ds(1, N_SEQ - 1)], 2)
    pos_all[0:1, :] = pos_send[0]
    for d in range(1, N_SEQ):
        pos_all[d : d + 1, :] = pos_recv[d]
    got = pos_all[...].astype(jnp.int32)
    spread = hot(iota((128, SLOTS), 0) == (iota((128, SLOTS), 1) & 31))
    mine = iota((N_SEQ, SLOTS), 0) == (iota((N_SEQ, SLOTS), 1) >> 5)
    row_hi = nn((got >> 4).astype(F32).astype(BF16), spread)
    row_lo = nn((got & 15).astype(F32).astype(BF16), spread)
    row = jnp.sum(jnp.where(mine, row_hi * 16.0 + row_lo, 0.0), axis=0, keepdims=True).astype(jnp.int32)
    for j in range(ROWS // 128):
        onehot_u[j * 128 : (j + 1) * 128, :] = hot(iota((128, SLOTS), 0) + j * 128 == row)
    row_b = jnp.broadcast_to(row.astype(F32), (128, SLOTS))
    for j in range(SLOTS // 128):
        col = jnp.transpose(row_b[:, j * 128 : (j + 1) * 128]).astype(jnp.int32)
        for k in range(ROWS // 128):
            onehot_ut[j * 128 : (j + 1) * 128, k * 128 : (k + 1) * 128] = hot(iota((128, 128), 1) + k * 128 == col)

    wait_recv(recv_a.at[others], 0)
    serial = nn(onehot_u[...], recv_a[...])
    center = serial - jnp.mean(serial, axis=1, keepdims=True)
    inv = lax.rsqrt(jnp.mean(center * center, axis=1, keepdims=True) + 1e-05)
    standard = center * inv
    xhat[...] = standard
    invs[...] = jnp.broadcast_to(inv, (ROWS, 128))
    normed_f = (standard * gain_ref[...]).astype(BF16)
    normed_t[...] = jnp.transpose(normed_f)
    qkv[...] = nn(normed_f, wqkv_ref[...]).astype(BF16)

    low = iota((ROWS, 128), 1) < HD

    def cols(base, p):
        return pl.ds(pl.multiple_of(base + p * 128, 128), 128)

    def half(x, h):
        return jnp.where(low if h == 0 else ~low, x.astype(F32), 0.0)

    def forward(p, _):
        q, k, v = qkv[:, cols(0, p)], qkv[:, cols(C, p)], qkv[:, cols(2 * C, p)]
        v_t = jnp.transpose(v)
        for h in range(2):
            scores = nt((half(k, h) * SCALE).astype(BF16), q)
            expo = jnp.exp(scores - jnp.max(scores, axis=0, keepdims=True))
            prob = expo * (1.0 / jnp.sum(expo, axis=0, keepdims=True))
            probs[2 * p + h] = prob
            rows = pl.ds(pl.multiple_of(p * 128 + h * HD, HD), HD)
            attn_t[rows, :] = nn(v_t[h * HD : (h + 1) * HD], prob.astype(BF16)).astype(BF16)
        return 0

    lax.fori_loop(0, PAIRS, forward, 0)

    wait_recv(recv_b.at[others], 1)
    sgrad[...] = nn(onehot_u[...], recv_b[...]).astype(BF16)
    dattn[...] = nt(sgrad[...], wproj_ref[...]).astype(BF16)

    def backward(p, _):
        q, k, v = qkv[:, cols(0, p)], qkv[:, cols(C, p)], qkv[:, cols(2 * C, p)]
        d_a = dattn[:, cols(0, p)]
        k_t = jnp.transpose(k)
        dq_t, dk, dv = [], [], []
        for h in range(2):
            prob = probs[2 * p + h]
            d_prob = nt(half(v, h).astype(BF16), d_a)
            delta = jnp.sum(d_prob * prob, axis=0, keepdims=True)
            d_score = (prob * (d_prob - delta) * SCALE).astype(BF16)
            dq_t.append(nn(k_t[h * HD : (h + 1) * HD], d_score))
            dk.append(nn(d_score, q))
            dv.append(nn(prob.astype(BF16), d_a))
        dq = jnp.transpose(jnp.concatenate(dq_t, axis=0)).astype(BF16)
        dk = jnp.where(low, dk[0], dk[1]).astype(BF16)
        dv = jnp.where(low, dv[0], dv[1]).astype(BF16)
        for n, part in enumerate((dq, dk, dv)):
            dqkv[:, cols(n * C, p)] = part
            grads_ref[p, n * C : (n + 1) * C, :] = nn(normed_t[...], part)
        proj = nn(attn_t[pl.ds(pl.multiple_of(p * 128, 128), 128), :], sgrad[...])
        for j in range(4):
            grads_ref[p, 3 * C + j * 128 : 3 * C + (j + 1) * 128, :] = proj[:, j * 128 : (j + 1) * 128]
        return 0

    lax.fori_loop(0, PAIRS, backward, 0)

    d_normed = nt(dqkv[...], wqkv_ref[...])
    standard = xhat[...]
    gg = jnp.sum(d_normed * standard, axis=0, keepdims=True)
    for j in range(8):
        gg_ref[j : j + 1, :] = gg[:, j * 128 : (j + 1) * 128] if j < 4 else jnp.zeros((1, 128), F32)
    scaled = d_normed * gain_ref[...]
    first = jnp.mean(scaled, axis=1, keepdims=True)
    second = jnp.mean(scaled * standard, axis=1, keepdims=True)
    dx = (sgrad[...].astype(F32) + invs[:, 0:1] * (scaled - first - standard * second)).astype(BF16)
    wait_send(send_a.at[others], 0)
    send_a[...] = nn(onehot_ut[...], dx).astype(BF16)
    back[0:CAP, :] = send_a[0:CAP, :]
    send_all(send_a, back, 3, -1)
    wait_recv(back.at[others], 3)
    out_ref[...] = nn(onehot_pt[...], back[...]).astype(BF16)
    wait_send(pos_recv.at[pl.ds(1, N_SEQ - 1)], 2)
    wait_send(send_b.at[others], 1)
    wait_send(send_a.at[others], 3)


AXES = {"seq_0": 4, "seq_1": 4, "seq_2": 2, "dp": 8}


def reduce_kernel(
    grads_ref, gg_ref, out_ref, gg_out_ref,
    res, acc, acc2, acc3, core_buf, first_buf, second_buf, z_buf, g_core, g_x, g_y, g_z,
    sem_send, sem_recv, g_send, g_recv, out_sem,
):
    me = {a: lax.axis_index(a) for a in AXES}

    def peers(axis):
        n = AXES[axis]
        return [lax.rem(me[axis] + d, n) for d in range(1, n)]

    barrier = pltpu.get_barrier_semaphore()
    for axis in AXES:
        for t in peers(axis):
            pl.semaphore_signal(barrier, inc=1, device_id={axis: t}, device_id_type=MESH_ID)
    pl.semaphore_wait(barrier, sum(n - 1 for n in AXES.values()))

    def order(p):
        return ("seq_0", "seq_1") if p % 2 == 0 else ("seq_1", "seq_0")

    def rows(start, n):
        return pl.ds(pl.multiple_of(start, 8), n)

    def wait_recv(ref, stage, p):
        remote(ref, ref, sem_send.at[stage, p], sem_recv.at[stage, p], dict(me)).wait_recv()

    def wait_send(ref, stage, p):
        remote(ref, ref, sem_send.at[stage, p], sem_recv.at[stage, p], dict(me)).wait_send()

    def send(src, dst, stage, p, axis, t):
        remote(src, dst, sem_send.at[stage, p], sem_recv.at[stage, p], {axis: t}).start()

    core = me["seq_2"]
    half = CHUNK // 2
    for p in range(PAIRS):
        send(grads_ref.at[p, rows((1 - core) * half, half)], core_buf.at[p], 0, p, "seq_2", 1 - core)

    def gain_stage(k, axis, buf, value):
        m, n = me[axis], AXES[axis]
        buf[m] = value
        for t in peers(axis):
            remote(buf.at[m], buf.at[m], g_send.at[k], g_recv.at[k], {axis: t}).start()

    def gain_sum(k, axis, buf):
        n = AXES[axis]
        ref = buf.at[pl.ds(0, n - 1)]
        copy = remote(ref, ref, g_send.at[k], g_recv.at[k], dict(me))
        copy.wait_recv()
        copy.wait_send()
        total = buf[0]
        for j in range(1, n):
            total = total + buf[j]
        return total

    gain_stage(0, "seq_2", g_core, gg_ref[...])
    for p in range(PAIRS):
        first = order(p)[0]
        wait_recv(core_buf.at[p], 0, p)
        acc[p] = grads_ref[p, rows(core * half, half), :] + core_buf[p]
        for d, t in enumerate(peers(first)):
            send(acc.at[p, rows(t * 256, 256)], first_buf.at[p, d], 1, p, first, t)
    gain_stage(1, "seq_0", g_x, gain_sum(0, "seq_2", g_core))
    for p in range(PAIRS):
        first, second = order(p)
        wait_recv(first_buf.at[p], 1, p)
        acc2[p] = acc[p, rows(me[first] * 256, 256), :] + first_buf[p, 0] + first_buf[p, 1] + first_buf[p, 2]
        for d, t in enumerate(peers(second)):
            send(acc2.at[p, rows(t * 64, 64)], second_buf.at[p, d], 2, p, second, t)
    gain_stage(2, "seq_1", g_y, gain_sum(1, "seq_0", g_x))
    for p in range(PAIRS):
        first, second = order(p)
        wait_recv(second_buf.at[p], 2, p)
        acc3[p] = acc2[p, rows(me[second] * 64, 64), :] + second_buf[p, 0] + second_buf[p, 1] + second_buf[p, 2]
        for d, t in enumerate(peers("dp")):
            send(acc3.at[p, rows(t * 8, 8)], z_buf.at[p, d], 3, p, "dp", t)
    gain_stage(3, "dp", g_z, gain_sum(2, "seq_1", g_y))
    base1, base2, base3 = [], [], []
    for p in range(PAIRS):
        first, second = order(p)
        base1.append(core * half + me[first] * 256)
        base2.append(base1[p] + me[second] * 64)
        base3.append(base2[p] + me["dp"] * 8)
        wait_recv(z_buf.at[p], 3, p)
        total = acc3[p, rows(me["dp"] * 8, 8), :]
        for d in range(7):
            total = total + z_buf[p, d]
        own = rows(base3[p], 8)
        res[p, own, :] = total
        for t in peers("dp"):
            send(res.at[p, own], res.at[p, own], 4, p, "dp", t)
    for p in range(PAIRS):
        second = order(p)[1]
        wait_recv(res.at[p, pl.ds(0, 56)], 4, p)
        own = rows(base2[p], 64)
        for t in peers(second):
            send(res.at[p, own], res.at[p, own], 5, p, second, t)
    for p in range(PAIRS):
        first = order(p)[0]
        wait_recv(res.at[p, pl.ds(0, 192)], 5, p)
        own = rows(base1[p], 256)
        for t in peers(first):
            send(res.at[p, own], res.at[p, own], 6, p, first, t)
    for p in range(PAIRS):
        wait_recv(res.at[p, pl.ds(0, 768)], 6, p)
        own = rows(core * half, half)
        send(res.at[p, own], res.at[p, own], 7, p, "seq_2", 1 - core)
    gg_out_ref[...] = gain_sum(3, "dp", g_z)
    for p in range(PAIRS):
        wait_recv(res.at[p, pl.ds(0, half)], 7, p)
        pltpu.make_async_copy(res.at[p], out_ref.at[p], out_sem.at[p]).start()
    sent = (half, 768, 192, 56, 56, 192, 768, half)
    for p in range(PAIRS):
        for stage in range(8):
            wait_send(res.at[p, pl.ds(0, sent[stage])], stage, p)
        pltpu.make_async_copy(res.at[p], out_ref.at[p], out_sem.at[p]).wait()


def vmem(shape, dtype=F32):
    return pltpu.VMEM(shape, dtype)


DMA = pltpu.SemaphoreType.DMA
VSPEC = pl.BlockSpec(memory_space=pltpu.VMEM)


def per_device(points, cotangent, dest, w_qkv, w_proj, gain):
    big = lambda: vmem((SLOTS, C), BF16)
    grad_local, grads, gg = pl.pallas_call(
        block_kernel,
        name="block",
        out_shape=(
            jax.ShapeDtypeStruct((ROWS, C), BF16),
            jax.ShapeDtypeStruct((PAIRS, CHUNK, 128), F32),
            jax.ShapeDtypeStruct((8, 128), F32),
        ),
        in_specs=[VSPEC] * 6,
        out_specs=(VSPEC,) * 3,
        scratch_shapes=[
            big(), big(), big(), big(), big(),
            vmem((N_SEQ, 1, 128)), vmem((N_SEQ, 1, 128)), vmem((N_SEQ, 128)),
            vmem((ROWS, 3 * C), BF16), vmem((ROWS, C), BF16), vmem((ROWS, C), BF16),
            vmem((ROWS, C)), vmem((ROWS, 128)), vmem((C, ROWS), BF16), vmem((ROWS, 3 * C), BF16),
            vmem((C, ROWS), BF16), vmem((HEADS, ROWS, ROWS)),
            vmem((ROWS, SLOTS), BF16), vmem((SLOTS, ROWS), BF16), vmem((ROWS, SLOTS), BF16),
            DMA((4,)), DMA((4,)),
        ],
        compiler_params=pltpu.CompilerParams(
            collective_id=0, has_side_effects=True, vmem_limit_bytes=56 * 2**20
        ),
    )(dest, points[0], cotangent[0], w_qkv, w_proj, gain[None, :])
    reduced, gg = pl.pallas_call(
        reduce_kernel,
        name="reduce",
        out_shape=(
            jax.ShapeDtypeStruct((PAIRS, CHUNK, 128), F32),
            jax.ShapeDtypeStruct((8, 128), F32),
        ),
        in_specs=[VSPEC] * 2,
        out_specs=(pl.BlockSpec(memory_space=pl.ANY), VSPEC),
        scratch_shapes=[
            vmem((PAIRS, CHUNK, 128)), vmem((PAIRS, CHUNK // 2, 128)), vmem((PAIRS, 256, 128)),
            vmem((PAIRS, 64, 128)), vmem((PAIRS, CHUNK // 2, 128)), vmem((PAIRS, 3, 256, 128)),
            vmem((PAIRS, 3, 64, 128)), vmem((PAIRS, 7, 8, 128)),
            vmem((2, 8, 128)), vmem((4, 8, 128)), vmem((4, 8, 128)), vmem((8, 8, 128)),
            DMA((8, PAIRS)), DMA((8, PAIRS)), DMA((4,)), DMA((4,)), DMA((PAIRS,)),
        ],
        compiler_params=pltpu.CompilerParams(
            collective_id=1, has_side_effects=True, vmem_limit_bytes=56 * 2**20
        ),
    )(grads, gg)
    parts = reduced.reshape(PAIRS, 4, C, 128)
    grad_qkv = jnp.transpose(parts[:, :3], (2, 1, 0, 3)).reshape(C, 3 * C)
    proj = parts[:, 3].reshape(PAIRS, 4, 128, 128)
    grad_proj = jnp.transpose(proj, (0, 2, 1, 3)).reshape(C, C)
    return (grad_local[None], grad_qkv, grad_proj, gg[:4].reshape(C))


def solution(mesh):
    finer = Mesh(mesh.devices.reshape(4, 4, 2, mesh.shape["dp"]), ("seq_0", "seq_1", "seq_2", "dp"))
    placed = (P("dp", SEQ, None), P("dp", SEQ, None), P("dp", SEQ), P(), P(), P())
    return jax.shard_map(
        per_device,
        mesh=finer,
        in_specs=placed,
        out_specs=(P("dp", SEQ, None), P(), P(), P()),
        check_vma=False,
    )
```

```python
import jax
import jax.numpy as jnp
from jax import lax
from jax.experimental import pallas as pl
from jax.experimental.pallas import tpu as pltpu
from jax.sharding import Mesh
from jax.sharding import PartitionSpec as P

SEQ = ("seq_0", "seq_1", "seq_2")
MESH_ID = pl.DeviceIdType.MESH
F32, BF16 = jnp.float32, jnp.bfloat16
ROWS = 512
C = 512
N_SEQ = 32
CAP = 32
SLOTS = N_SEQ * CAP
HEADS, HD = 8, 64
PAIRS = HEADS // 2
SCALE = 1.0 / HD**0.5
CHUNK = 2048


def nn(a, b):
    return jnp.dot(a, b, preferred_element_type=F32)


def nt(a, b):
    return lax.dot_general(a, b, (((1,), (1,)), ((), ())), preferred_element_type=F32)


def iota(shape, dim):
    return lax.broadcasted_iota(jnp.int32, shape, dim)


def hot(cond):
    return jnp.where(cond, 1.0, 0.0).astype(BF16)


def remote(src, dst, send, recv, device):
    return pltpu.make_async_remote_copy(
        src_ref=src, dst_ref=dst, send_sem=send, recv_sem=recv, device_id=device, device_id_type=MESH_ID
    )


def seq_peer(mx, my, mc, d, sign):
    dx, dy, dc = d // 8, (d // 2) % 4, d % 2
    return {
        "seq_0": lax.rem(mx + (dx if sign > 0 else 4 - dx), 4),
        "seq_1": lax.rem(my + (dy if sign > 0 else 4 - dy), 4),
        "seq_2": lax.rem(mc + dc, 2),
    }


AXES = {"seq_0": 4, "seq_1": 4, "seq_2": 2, "dp": 8}
FAR_FIRST = sorted(range(1, N_SEQ), key=lambda d: -(min(d // 8, 4 - d // 8) + min(d // 2 % 4, 4 - d // 2 % 4)))


def block_kernel(
    dest_ref, pts_hbm, cot_hbm, wqkv_hbm, wproj_hbm, gain_ref,
    out_ref, res, gg_ref,
    send_a, recv_a, send_b, recv_b, back, pos_send, pos_recv, pos_all,
    qkv, dattn, sgrad, xhat, invs, normed_t, dqkv, attn_t, probs, onehot_u, onehot_ut, onehot_pt,
    grads, acc, acc2, acc3, core_buf, first_buf, second_buf, z_buf, g_core, g_x, g_y, g_z,
    pts_ref, cot_ref, wqkv_ref, wproj_ref,
    sem_send, sem_recv, r_send, r_recv, g_send, g_recv, in_sem,
):
    loads = [
        pltpu.make_async_copy(src, dst, in_sem.at[k])
        for k, (src, dst) in enumerate(
            ((pts_hbm, pts_ref), (cot_hbm, cot_ref), (wqkv_hbm, wqkv_ref), (wproj_hbm, wproj_ref))
        )
    ]
    for load in loads:
        load.start()
    me = {a: lax.axis_index(a) for a in AXES}
    mx, my, mc = me["seq_0"], me["seq_1"], me["seq_2"]
    here = dict(me)

    def peers(axis):
        n = AXES[axis]
        return [lax.rem(me[axis] + d, n) for d in range(1, n)]

    barrier = pltpu.get_barrier_semaphore()
    for d in range(1, N_SEQ):
        pl.semaphore_signal(barrier, inc=1, device_id=seq_peer(mx, my, mc, d, 1), device_id_type=MESH_ID)
    for t in peers("dp"):
        pl.semaphore_signal(barrier, inc=1, device_id={"dp": t}, device_id_type=MESH_ID)

    dest = dest_ref[...]
    owner, slot = dest >> 9, dest & 511
    rel = ((((owner >> 3) - mx) & 3) << 3) | ((((owner >> 1) - my) & 3) << 1) | ((owner - mc) & 1)
    to_hot_f = jnp.where(iota((N_SEQ, ROWS), 0) == rel, 1.0, 0.0)
    to_hot = to_hot_f.astype(BF16)
    earlier = hot(iota((ROWS, ROWS), 0) < iota((ROWS, ROWS), 1))
    rank = jnp.sum(to_hot_f * nn(to_hot, earlier), axis=0, keepdims=True).astype(jnp.int32)
    sid = rel * CAP + rank
    rank_hot = hot(iota((128, ROWS), 0) == rank)
    pos_hi = nt((to_hot_f * (slot >> 4).astype(F32)).astype(BF16), rank_hot)
    pos_lo = nt((to_hot_f * (slot & 15).astype(F32)).astype(BF16), rank_hot)
    pos = pos_hi * 16.0 + pos_lo
    for d in range(N_SEQ):
        pos_send[d] = pos[d : d + 1, :]

    def pack(src_ref, send_ref, recv_ref, index, first=None):
        data = src_ref[...]
        for b in (2, 1, 3, 0):
            pick = hot(iota((256, ROWS), 0) + b * 256 == sid)
            send_ref[b * 256 : (b + 1) * 256, :] = nn(pick, data).astype(BF16)
            if first is not None:
                first()
                first = None
            send_all(send_ref, recv_ref, index, 1, [d for d in FAR_FIRST if d // 8 == b])
        recv_ref[0:CAP, :] = send_ref[0:CAP, :]

    def send_all(send_ref, recv_ref, index, sign, order=FAR_FIRST):
        for d in order:
            rows = pl.ds(d * CAP, CAP)
            remote(send_ref.at[rows], recv_ref.at[rows], sem_send.at[index], sem_recv.at[index],
                   seq_peer(mx, my, mc, d, sign)).start()

    def wait_recv(ref, index):
        remote(ref, ref, sem_send.at[index], sem_recv.at[index], here).wait_recv()

    def wait_send(ref, index):
        remote(ref, ref, sem_send.at[index], sem_recv.at[index], here).wait_send()

    def enter():
        pl.semaphore_wait(barrier, N_SEQ - 1 + AXES["dp"] - 1)
        for d in range(1, N_SEQ):
            remote(pos_send.at[d], pos_recv.at[d], sem_send.at[2], sem_recv.at[2],
                   seq_peer(mx, my, mc, d, 1)).start()

    loads[0].wait()
    pack(pts_ref, send_a, recv_a, 0, enter)
    loads[1].wait()
    pack(cot_ref, send_b, recv_b, 1)

    sid_col = jnp.transpose(jnp.broadcast_to(sid.astype(F32), (128, ROWS))).astype(jnp.int32)
    for j in range(SLOTS // 128):
        onehot_pt[:, j * 128 : (j + 1) * 128] = hot(iota((ROWS, 128), 1) + j * 128 == sid_col)

    others = pl.ds(CAP, SLOTS - CAP)
    wait_recv(pos_recv.at[pl.ds(1, N_SEQ - 1)], 2)
    pos_all[0:1, :] = pos_send[0]
    for d in range(1, N_SEQ):
        pos_all[d : d + 1, :] = pos_recv[d]
    got = pos_all[...].astype(jnp.int32)
    spread = hot(iota((128, SLOTS), 0) == (iota((128, SLOTS), 1) & 31))
    mine = iota((N_SEQ, SLOTS), 0) == (iota((N_SEQ, SLOTS), 1) >> 5)
    row_hi = nn((got >> 4).astype(F32).astype(BF16), spread)
    row_lo = nn((got & 15).astype(F32).astype(BF16), spread)
    row = jnp.sum(jnp.where(mine, row_hi * 16.0 + row_lo, 0.0), axis=0, keepdims=True).astype(jnp.int32)
    for j in range(ROWS // 128):
        onehot_u[j * 128 : (j + 1) * 128, :] = hot(iota((128, SLOTS), 0) + j * 128 == row)
    row_b = jnp.broadcast_to(row.astype(F32), (128, SLOTS))
    for j in range(SLOTS // 128):
        col = jnp.transpose(row_b[:, j * 128 : (j + 1) * 128]).astype(jnp.int32)
        for k in range(ROWS // 128):
            onehot_ut[j * 128 : (j + 1) * 128, k * 128 : (k + 1) * 128] = hot(iota((128, 128), 1) + k * 128 == col)

    wait_recv(recv_a.at[others], 0)
    serial = nn(onehot_u[...], recv_a[...])
    center = serial - jnp.mean(serial, axis=1, keepdims=True)
    inv = lax.rsqrt(jnp.mean(center * center, axis=1, keepdims=True) + 1e-05)
    standard = center * inv
    xhat[...] = standard
    invs[...] = jnp.broadcast_to(inv, (ROWS, 128))
    normed_f = (standard * gain_ref[...]).astype(BF16)
    normed_t[...] = jnp.transpose(normed_f)
    loads[2].wait()
    qkv[...] = nn(normed_f, wqkv_ref[...]).astype(BF16)

    low = iota((ROWS, 128), 1) < HD

    def cols(base, p):
        return pl.ds(pl.multiple_of(base + p * 128, 128), 128)

    def half(x, h):
        return jnp.where(low if h == 0 else ~low, x.astype(F32), 0.0)

    def forward(p, _):
        q, k, v = qkv[:, cols(0, p)], qkv[:, cols(C, p)], qkv[:, cols(2 * C, p)]
        v_t = jnp.transpose(v)
        for h in range(2):
            scores = nt((half(k, h) * SCALE).astype(BF16), q)
            expo = jnp.exp(scores - jnp.max(scores, axis=0, keepdims=True))
            prob = expo * (1.0 / jnp.sum(expo, axis=0, keepdims=True))
            probs[2 * p + h] = prob
            rows = pl.ds(pl.multiple_of(p * 128 + h * HD, HD), HD)
            attn_t[rows, :] = nn(v_t[h * HD : (h + 1) * HD], prob.astype(BF16)).astype(BF16)
        return 0

    lax.fori_loop(0, PAIRS, forward, 0)

    wait_recv(recv_b.at[others], 1)
    sgrad[...] = nn(onehot_u[...], recv_b[...]).astype(BF16)
    loads[3].wait()
    dattn[...] = nt(sgrad[...], wproj_ref[...]).astype(BF16)

    def values_part(c, hook):
        for k in range(2):
            p = 2 * c + k
            at = slice(p * 128, (p + 1) * 128)
            dv = [nn(probs[2 * p + h].astype(BF16), dattn[:, at]) for h in range(2)]
            dv = jnp.where(low, dv[0], dv[1]).astype(BF16)
            dqkv[:, 2 * C + p * 128 : 2 * C + (p + 1) * 128] = dv
            grads[c, k * C : (k + 1) * C, :] = nn(normed_t[...], dv)
            if k == 0:
                hook()
            proj = nn(attn_t[at, :], sgrad[...])
            for j in range(4):
                grads[c, (2 + k) * C + j * 128 : (2 + k) * C + (j + 1) * 128, :] = proj[:, j * 128 : (j + 1) * 128]

    def keys_part(c, hook):
        for k in range(2):
            p = 2 * c + k
            at = slice(p * 128, (p + 1) * 128)
            q, keys, v = qkv[:, at], qkv[:, C + p * 128 : C + (p + 1) * 128], qkv[:, 2 * C + p * 128 : 2 * C + (p + 1) * 128]
            k_t = jnp.transpose(keys)
            dq_t, dk = [], []
            for h in range(2):
                prob = probs[2 * p + h]
                d_prob = nt(half(v, h).astype(BF16), dattn[:, at])
                delta = jnp.sum(d_prob * prob, axis=0, keepdims=True)
                d_score = (prob * (d_prob - delta) * SCALE).astype(BF16)
                dq_t.append(nn(k_t[h * HD : (h + 1) * HD], d_score))
                dk.append(nn(d_score, q))
            dq = jnp.transpose(jnp.concatenate(dq_t, axis=0)).astype(BF16)
            dk = jnp.where(low, dk[0], dk[1]).astype(BF16)
            for n, part in enumerate((dq, dk)):
                dqkv[:, n * C + p * 128 : n * C + (p + 1) * 128] = part
                grads[2 + c, (2 * k + n) * C : (2 * k + n + 1) * C, :] = nn(normed_t[...], part)
            if k == 0:
                hook()

    def span(start, n):
        return pl.ds(pl.multiple_of(start, 8), n)

    core = me["seq_2"]
    half_rows = CHUNK // 2
    COLORS = (("seq_0", "seq_1"), ("seq_1", "seq_0"))

    def place(color, level):
        first, second = COLORS[color]
        at = core * half_rows + color * 512
        if level > 0:
            at = at + me[first] * 128
        if level > 1:
            at = at + me[second] * 32
        return at

    def r_wait_recv(ref, stage, p):
        remote(ref, ref, r_send.at[stage, p], r_recv.at[stage, p], here).wait_recv()

    def r_wait_send(ref, stage, p):
        remote(ref, ref, r_send.at[stage, p], r_recv.at[stage, p], here).wait_send()

    def r_start(src, dst, stage, p, axis, t):
        remote(src, dst, r_send.at[stage, p], r_recv.at[stage, p], {axis: t}).start()

    def s_core(p):
        r_start(grads.at[p, span((1 - core) * half_rows, half_rows)], core_buf.at[p], 0, p, "seq_2", 1 - core)

    def s_first(p):
        r_wait_recv(core_buf.at[p], 0, p)
        acc[p] = grads[p, span(core * half_rows, half_rows), :] + core_buf[p]
        for d in range(3):
            for color, (first, _) in enumerate(COLORS):
                t = peers(first)[d]
                r_start(acc.at[p, span(color * 512 + t * 128, 128)], first_buf.at[p, color, d], 1, p, first, t)

    def s_second(p):
        r_wait_recv(first_buf.at[p], 1, p)
        for color, (first, _) in enumerate(COLORS):
            got = first_buf[p, color, 0] + first_buf[p, color, 1] + first_buf[p, color, 2]
            acc2[p, color * 128 : (color + 1) * 128, :] = acc[p, span(color * 512 + me[first] * 128, 128), :] + got
        for d in range(3):
            for color, (_, second) in enumerate(COLORS):
                t = peers(second)[d]
                r_start(acc2.at[p, span(color * 128 + t * 32, 32)], second_buf.at[p, color, d], 2, p, second, t)

    def s_z(p):
        r_wait_recv(second_buf.at[p], 2, p)
        for color, (_, second) in enumerate(COLORS):
            got = second_buf[p, color, 0] + second_buf[p, color, 1] + second_buf[p, color, 2]
            acc3[p, color * 32 : (color + 1) * 32, :] = acc2[p, span(color * 128 + me[second] * 32, 32), :] + got
        for d, t in enumerate(peers("dp")):
            r_start(acc3.at[p, span(t * 8, 8)], z_buf.at[p, d], 3, p, "dp", t)

    z = me["dp"]
    z_color, z_block = z // 4, lax.rem(z, 4)
    z_place = (1 - z_color) * place(0, 2) + z_color * place(1, 2) + z_block * 8

    def s_gather_z(p):
        r_wait_recv(z_buf.at[p], 3, p)
        total = acc3[p, span(z * 8, 8), :]
        for d in range(7):
            total = total + z_buf[p, d]
        own = span(z_place, 8)
        res[p, own, :] = total.astype(BF16)
        for t in peers("dp"):
            r_start(res.at[p, own], res.at[p, own], 4, p, "dp", t)

    def s_gather_second(p):
        r_wait_recv(res.at[p, pl.ds(0, 56)], 4, p)
        for d in range(3):
            for color, (_, second) in enumerate(COLORS):
                own = span(place(color, 2), 32)
                r_start(res.at[p, own], res.at[p, own], 5, p, second, peers(second)[d])

    def s_gather_first(p):
        r_wait_recv(res.at[p, pl.ds(0, 192)], 5, p)
        for d in range(3):
            for color, (first, _) in enumerate(COLORS):
                own = span(place(color, 1), 128)
                r_start(res.at[p, own], res.at[p, own], 6, p, first, peers(first)[d])

    def s_gather_core(p):
        r_wait_recv(res.at[p, pl.ds(0, 768)], 6, p)
        own = span(core * half_rows, half_rows)
        r_start(res.at[p, own], res.at[p, own], 7, p, "seq_2", 1 - core)

    def finish(p):
        r_wait_recv(res.at[p, pl.ds(0, half_rows)], 7, p)

    def gain_stage(k, axis, buf, value):
        m = me[axis]
        buf[m] = value
        for t in peers(axis):
            remote(buf.at[m], buf.at[m], g_send.at[k], g_recv.at[k], {axis: t}).start()

    def gain_sum(k, axis, buf):
        n = AXES[axis]
        ref = buf.at[pl.ds(0, n - 1)]
        copy = remote(ref, ref, g_send.at[k], g_recv.at[k], here)
        copy.wait_recv()
        copy.wait_send()
        total = buf[0]
        for j in range(1, n):
            total = total + buf[j]
        return total

    values_part(0, lambda: None)
    s_core(0)
    values_part(1, lambda: s_first(0))
    s_core(1)
    keys_part(0, lambda: s_first(1))
    s_core(2)
    keys_part(1, lambda: s_first(2))
    s_core(3)

    d_normed = nt(dqkv[...], wqkv_ref[...])
    s_first(3)
    standard = xhat[...]
    gg = jnp.sum(d_normed * standard, axis=0, keepdims=True)
    for j in range(8):
        gg_ref[j : j + 1, :] = gg[:, j * 128 : (j + 1) * 128] if j < 4 else jnp.zeros((1, 128), F32)
    gain_stage(0, "seq_2", g_core, gg_ref[...])
    scaled = d_normed * gain_ref[...]
    first = jnp.mean(scaled, axis=1, keepdims=True)
    second = jnp.mean(scaled * standard, axis=1, keepdims=True)
    dx = (sgrad[...].astype(F32) + invs[:, 0:1] * (scaled - first - standard * second)).astype(BF16)
    wait_send(send_a.at[others], 0)
    send_a[...] = nn(onehot_ut[...], dx).astype(BF16)
    back[0:CAP, :] = send_a[0:CAP, :]
    gain_stage(1, "seq_0", g_x, gain_sum(0, "seq_2", g_core))
    for p in range(PAIRS):
        s_second(p)
    send_all(send_a, back, 3, -1, FAR_FIRST[:8])
    for p in range(PAIRS):
        s_z(p)
    send_all(send_a, back, 3, -1, FAR_FIRST[8:18])
    gain_stage(2, "seq_1", g_y, gain_sum(1, "seq_0", g_x))
    for p in range(PAIRS):
        s_gather_z(p)
    send_all(send_a, back, 3, -1, FAR_FIRST[18:28])
    for p in range(PAIRS):
        s_gather_second(p)
    send_all(send_a, back, 3, -1, FAR_FIRST[28:])
    gain_stage(3, "dp", g_z, gain_sum(2, "seq_1", g_y))
    for p in range(PAIRS):
        s_gather_first(p)
    for p in range(PAIRS):
        s_gather_core(p)
    wait_recv(back.at[others], 3)
    out_ref[...] = nn(onehot_pt[...], back[...]).astype(BF16)
    gg_ref[...] = gain_sum(3, "dp", g_z)
    for p in range(PAIRS):
        finish(p)
    wait_send(pos_recv.at[pl.ds(1, N_SEQ - 1)], 2)
    wait_send(send_b.at[others], 1)
    wait_send(send_a.at[others], 3)
    sent = (half_rows, 768, 192, 56, 56, 192, 768, half_rows)
    for p in range(PAIRS):
        for stage in range(8):
            r_wait_send((grads if stage < 4 else res).at[p, pl.ds(0, sent[stage])], stage, p)


def vmem(shape, dtype=F32):
    return pltpu.VMEM(shape, dtype)


DMA = pltpu.SemaphoreType.DMA
VSPEC = pl.BlockSpec(memory_space=pltpu.VMEM)
HBM = pl.BlockSpec(memory_space=pltpu.HBM)


def widen_kernel(res_ref, rows_ref, gg_ref, pts_out, qkv_out, proj_out, gain_out, wide, wide_p, sem):
    copies = [pltpu.make_async_copy(rows_ref, pts_out.at[0], sem.at[0])]
    copies[0].start()
    for r in range(4):
        at = slice(r * 128, (r + 1) * 128)
        for p in range(PAIRS):
            lanes = slice(p * 128, (p + 1) * 128)
            c, k = p // 2, p % 2
            for n, (chunk, row) in enumerate(((2 + c, 2 * k), (2 + c, 2 * k + 1), (c, k))):
                start = row * C + r * 128
                wide[at, n * C + p * 128 : n * C + (p + 1) * 128] = res_ref[chunk, start : start + 128, :].astype(F32)
            start = (2 + r % 2) * C + p * 128
            wide_p[at, lanes] = res_ref[r // 2, start : start + 128, :].astype(F32)
        rows = pl.ds(r * 128, 128)
        copies.append(pltpu.make_async_copy(wide.at[rows], qkv_out.at[rows], sem.at[1 + r]))
        copies.append(pltpu.make_async_copy(wide_p.at[rows], proj_out.at[rows], sem.at[5 + r]))
        copies[-2].start()
        copies[-1].start()
    for j in range(4):
        gain_out[:, j * 128 : (j + 1) * 128] = gg_ref[j : j + 1, :]
    for copy in copies:
        copy.wait()


def per_device(points, cotangent, dest, w_qkv, w_proj, gain):
    big = lambda: vmem((SLOTS, C), BF16)
    grad_local, res, gg = pl.pallas_call(
        block_kernel,
        name="block",
        out_shape=(
            vmem((ROWS, C), BF16),
            vmem((PAIRS, CHUNK, 128), BF16),
            vmem((8, 128)),
        ),
        in_specs=[VSPEC, HBM, HBM, HBM, HBM, VSPEC],
        out_specs=(VSPEC,) * 3,
        scratch_shapes=[
            big(), big(), big(), big(), big(),
            vmem((N_SEQ, 1, 128)), vmem((N_SEQ, 1, 128)), vmem((N_SEQ, 128)),
            vmem((ROWS, 3 * C), BF16), vmem((ROWS, C), BF16), vmem((ROWS, C), BF16),
            vmem((ROWS, C)), vmem((ROWS, 128)), vmem((C, ROWS), BF16), vmem((ROWS, 3 * C), BF16),
            vmem((C, ROWS), BF16), vmem((HEADS, ROWS, ROWS)),
            vmem((ROWS, SLOTS), BF16), vmem((SLOTS, ROWS), BF16), vmem((ROWS, SLOTS), BF16),
            vmem((PAIRS, CHUNK, 128)), vmem((PAIRS, CHUNK // 2, 128)),
            vmem((PAIRS, 256, 128)), vmem((PAIRS, 64, 128)), vmem((PAIRS, CHUNK // 2, 128)),
            vmem((PAIRS, 2, 3, 128, 128)), vmem((PAIRS, 2, 3, 32, 128)), vmem((PAIRS, 7, 8, 128)),
            vmem((2, 8, 128)), vmem((4, 8, 128)), vmem((4, 8, 128)), vmem((8, 8, 128)),
            vmem((ROWS, C), BF16), vmem((ROWS, C), BF16), vmem((C, 3 * C), BF16), vmem((C, C), BF16),
            DMA((4,)), DMA((4,)), DMA((8, PAIRS)), DMA((8, PAIRS)), DMA((4,)), DMA((4,)), DMA((4,)),
        ],
        compiler_params=pltpu.CompilerParams(
            collective_id=0, has_side_effects=True, vmem_limit_bytes=56 * 2**20
        ),
    )(dest, points[0], cotangent[0], w_qkv, w_proj, gain[None, :])
    grad_points, grad_qkv, grad_proj, gain_gradient = pl.pallas_call(
        widen_kernel,
        name="widen",
        out_shape=(
            jax.ShapeDtypeStruct((1, ROWS, C), BF16),
            jax.ShapeDtypeStruct((C, 3 * C), F32),
            jax.ShapeDtypeStruct((C, C), F32),
            jax.ShapeDtypeStruct((1, C), F32),
        ),
        in_specs=[VSPEC] * 3,
        out_specs=(HBM, HBM, HBM, VSPEC),
        scratch_shapes=[vmem((C, 3 * C)), vmem((C, C)), DMA((9,))],
        compiler_params=pltpu.CompilerParams(vmem_limit_bytes=16 * 2**20),
    )(res, grad_local, gg)
    return (grad_points, grad_qkv, grad_proj, gain_gradient.reshape(C))


def solution(mesh):
    finer = Mesh(mesh.devices.reshape(4, 4, 2, mesh.shape["dp"]), ("seq_0", "seq_1", "seq_2", "dp"))
    placed = (P("dp", SEQ, None), P("dp", SEQ, None), P("dp", SEQ), P(), P(), P())
    return jax.shard_map(
        per_device,
        mesh=finer,
        in_specs=placed,
        out_specs=(P("dp", SEQ, None), P(), P(), P()),
        check_vma=False,
    )
```

```python
import jax
import jax.numpy as jnp
from jax import lax
from jax.experimental import pallas as pl
from jax.experimental.pallas import tpu as pltpu
from jax.sharding import Mesh
from jax.sharding import PartitionSpec as P

SEQ = ("seq_0", "seq_1", "seq_2")
MESH_ID = pl.DeviceIdType.MESH
F32, BF16 = jnp.float32, jnp.bfloat16
ROWS = 512
C = 512
N_SEQ = 32
CAP = 32
SLOTS = N_SEQ * CAP
HEADS, HD = 8, 64
PAIRS = HEADS // 2
SCALE = 1.0 / HD**0.5
CHUNK = 2048


def nn(a, b):
    return jnp.dot(a, b, preferred_element_type=F32)


def nt(a, b):
    return lax.dot_general(a, b, (((1,), (1,)), ((), ())), preferred_element_type=F32)


def iota(shape, dim):
    return lax.broadcasted_iota(jnp.int32, shape, dim)


def hot(cond):
    return jnp.where(cond, 1.0, 0.0).astype(BF16)


def remote(src, dst, send, recv, device):
    return pltpu.make_async_remote_copy(
        src_ref=src, dst_ref=dst, send_sem=send, recv_sem=recv, device_id=device, device_id_type=MESH_ID
    )


def seq_peer(mx, my, mc, d, sign):
    dx, dy, dc = d // 8, (d // 2) % 4, d % 2
    return {
        "seq_0": lax.rem(mx + (dx if sign > 0 else 4 - dx), 4),
        "seq_1": lax.rem(my + (dy if sign > 0 else 4 - dy), 4),
        "seq_2": lax.rem(mc + dc, 2),
    }


AXES = {"seq_0": 4, "seq_1": 4, "seq_2": 2, "dp": 8}
FAR_FIRST = sorted(range(1, N_SEQ), key=lambda d: -(min(d // 8, 4 - d // 8) + min(d // 2 % 4, 4 - d // 2 % 4)))


def block_kernel(
    dest_ref, pts_hbm, cot_hbm, wqkv_hbm, wproj_hbm, gain_ref,
    out_ref, res, gg_ref,
    send_a, recv_a, send_b, recv_b, back, pos_send, pos_recv, pos_all,
    qkv, dattn, sgrad, xhat, invs, normed_t, dqkv, attn_t, probs, onehot_u, onehot_ut, onehot_pt,
    grads, acc, acc2, acc3, core_buf, first_buf, second_buf, z_buf, g_core, g_x, g_y, g_z,
    pts_ref, cot_ref, wqkv_ref, wproj_ref,
    sem_send, sem_recv, r_send, r_recv, g_send, g_recv, in_sem,
):
    loads = [
        pltpu.make_async_copy(src, dst, in_sem.at[k])
        for k, (src, dst) in enumerate(
            ((pts_hbm, pts_ref), (cot_hbm, cot_ref), (wqkv_hbm, wqkv_ref), (wproj_hbm, wproj_ref))
        )
    ]
    for load in loads:
        load.start()
    me = {a: lax.axis_index(a) for a in AXES}
    mx, my, mc = me["seq_0"], me["seq_1"], me["seq_2"]
    here = dict(me)

    def peers(axis):
        n = AXES[axis]
        return [lax.rem(me[axis] + d, n) for d in range(1, n)]

    barrier = pltpu.get_barrier_semaphore()
    for d in range(1, N_SEQ):
        pl.semaphore_signal(barrier, inc=1, device_id=seq_peer(mx, my, mc, d, 1), device_id_type=MESH_ID)
    for t in peers("dp"):
        pl.semaphore_signal(barrier, inc=1, device_id={"dp": t}, device_id_type=MESH_ID)

    dest = dest_ref[...]
    owner, slot = dest >> 9, dest & 511
    rel = ((((owner >> 3) - mx) & 3) << 3) | ((((owner >> 1) - my) & 3) << 1) | ((owner - mc) & 1)
    to_hot_f = jnp.where(iota((N_SEQ, ROWS), 0) == rel, 1.0, 0.0)
    to_hot = to_hot_f.astype(BF16)
    earlier = hot(iota((ROWS, ROWS), 0) < iota((ROWS, ROWS), 1))
    rank = jnp.sum(to_hot_f * nn(to_hot, earlier), axis=0, keepdims=True).astype(jnp.int32)
    sid = rel * CAP + rank
    rank_hot = hot(iota((128, ROWS), 0) == rank)
    pos_hi = nt((to_hot_f * (slot >> 4).astype(F32)).astype(BF16), rank_hot)
    pos_lo = nt((to_hot_f * (slot & 15).astype(F32)).astype(BF16), rank_hot)
    pos = pos_hi * 16.0 + pos_lo
    for d in range(N_SEQ):
        pos_send[d] = pos[d : d + 1, :]

    def pack(src_ref, send_ref, recv_ref, index, first=None):
        data = src_ref[...]
        for b in (2, 1, 3, 0):
            pick = hot(iota((256, ROWS), 0) + b * 256 == sid)
            send_ref[b * 256 : (b + 1) * 256, :] = nn(pick, data).astype(BF16)
            if first is not None:
                first()
                first = None
            send_all(send_ref, recv_ref, index, 1, [d for d in FAR_FIRST if d // 8 == b])
        recv_ref[0:CAP, :] = send_ref[0:CAP, :]

    def send_all(send_ref, recv_ref, index, sign, order=FAR_FIRST):
        for d in order:
            rows = pl.ds(d * CAP, CAP)
            remote(send_ref.at[rows], recv_ref.at[rows], sem_send.at[index], sem_recv.at[index],
                   seq_peer(mx, my, mc, d, sign)).start()

    def wait_recv(ref, index):
        remote(ref, ref, sem_send.at[index], sem_recv.at[index], here).wait_recv()

    def wait_send(ref, index):
        remote(ref, ref, sem_send.at[index], sem_recv.at[index], here).wait_send()

    def enter():
        pl.semaphore_wait(barrier, N_SEQ - 1 + AXES["dp"] - 1)
        for d in range(1, N_SEQ):
            remote(pos_send.at[d], pos_recv.at[d], sem_send.at[2], sem_recv.at[2],
                   seq_peer(mx, my, mc, d, 1)).start()

    loads[0].wait()
    pack(pts_ref, send_a, recv_a, 0, enter)
    loads[1].wait()
    pack(cot_ref, send_b, recv_b, 1)

    sid_col = jnp.transpose(jnp.broadcast_to(sid.astype(F32), (128, ROWS))).astype(jnp.int32)
    for j in range(SLOTS // 128):
        onehot_pt[:, j * 128 : (j + 1) * 128] = hot(iota((ROWS, 128), 1) + j * 128 == sid_col)

    others = pl.ds(CAP, SLOTS - CAP)
    wait_recv(pos_recv.at[pl.ds(1, N_SEQ - 1)], 2)
    pos_all[0:1, :] = pos_send[0]
    for d in range(1, N_SEQ):
        pos_all[d : d + 1, :] = pos_recv[d]
    got = pos_all[...].astype(jnp.int32)
    spread = hot(iota((128, SLOTS), 0) == (iota((128, SLOTS), 1) & 31))
    mine = iota((N_SEQ, SLOTS), 0) == (iota((N_SEQ, SLOTS), 1) >> 5)
    row_hi = nn((got >> 4).astype(F32).astype(BF16), spread)
    row_lo = nn((got & 15).astype(F32).astype(BF16), spread)
    row = jnp.sum(jnp.where(mine, row_hi * 16.0 + row_lo, 0.0), axis=0, keepdims=True).astype(jnp.int32)
    for j in range(ROWS // 128):
        onehot_u[j * 128 : (j + 1) * 128, :] = hot(iota((128, SLOTS), 0) + j * 128 == row)
    row_b = jnp.broadcast_to(row.astype(F32), (128, SLOTS))
    for j in range(SLOTS // 128):
        col = jnp.transpose(row_b[:, j * 128 : (j + 1) * 128]).astype(jnp.int32)
        for k in range(ROWS // 128):
            onehot_ut[j * 128 : (j + 1) * 128, k * 128 : (k + 1) * 128] = hot(iota((128, 128), 1) + k * 128 == col)

    wait_recv(recv_a.at[others], 0)
    serial = nn(onehot_u[...], recv_a[...])
    center = serial - jnp.mean(serial, axis=1, keepdims=True)
    inv = lax.rsqrt(jnp.mean(center * center, axis=1, keepdims=True) + 1e-05)
    standard = center * inv
    xhat[...] = standard
    invs[...] = jnp.broadcast_to(inv, (ROWS, 128))
    normed_f = (standard * gain_ref[...]).astype(BF16)
    normed_t[...] = jnp.transpose(normed_f)
    loads[2].wait()
    qkv[...] = nn(normed_f, wqkv_ref[...]).astype(BF16)

    low = iota((ROWS, 128), 1) < HD

    def cols(base, p):
        return pl.ds(pl.multiple_of(base + p * 128, 128), 128)

    def half(x, h):
        return jnp.where(low if h == 0 else ~low, x.astype(F32), 0.0)

    def forward(p, _):
        q, k, v = qkv[:, cols(0, p)], qkv[:, cols(C, p)], qkv[:, cols(2 * C, p)]
        v_t = jnp.transpose(v)
        for h in range(2):
            scores = nt((half(k, h) * SCALE).astype(BF16), q)
            expo = jnp.exp(scores - jnp.max(scores, axis=0, keepdims=True))
            prob = expo * (1.0 / jnp.sum(expo, axis=0, keepdims=True))
            probs[2 * p + h] = prob
            rows = pl.ds(pl.multiple_of(p * 128 + h * HD, HD), HD)
            attn_t[rows, :] = nn(v_t[h * HD : (h + 1) * HD], prob.astype(BF16)).astype(BF16)
        return 0

    lax.fori_loop(0, PAIRS, forward, 0)

    wait_recv(recv_b.at[others], 1)
    sgrad[...] = nn(onehot_u[...], recv_b[...]).astype(BF16)
    loads[3].wait()
    dattn[...] = nt(sgrad[...], wproj_ref[...]).astype(BF16)

    def values_part(c, hook):
        for k in range(2):
            p = 2 * c + k
            at = slice(p * 128, (p + 1) * 128)
            dv = [nn(probs[2 * p + h].astype(BF16), dattn[:, at]) for h in range(2)]
            dv = jnp.where(low, dv[0], dv[1]).astype(BF16)
            dqkv[:, 2 * C + p * 128 : 2 * C + (p + 1) * 128] = dv
            grads[c, k * C : (k + 1) * C, :] = nn(normed_t[...], dv)
            if k == 0:
                hook()
            proj = nn(attn_t[at, :], sgrad[...])
            for j in range(4):
                grads[c, (2 + k) * C + j * 128 : (2 + k) * C + (j + 1) * 128, :] = proj[:, j * 128 : (j + 1) * 128]

    def keys_part(c, hook):
        for k in range(2):
            p = 2 * c + k
            at = slice(p * 128, (p + 1) * 128)
            q, keys, v = qkv[:, at], qkv[:, C + p * 128 : C + (p + 1) * 128], qkv[:, 2 * C + p * 128 : 2 * C + (p + 1) * 128]
            k_t = jnp.transpose(keys)
            dq_t, dk = [], []
            for h in range(2):
                prob = probs[2 * p + h]
                d_prob = nt(half(v, h).astype(BF16), dattn[:, at])
                delta = jnp.sum(d_prob * prob, axis=0, keepdims=True)
                d_score = (prob * (d_prob - delta) * SCALE).astype(BF16)
                dq_t.append(nn(k_t[h * HD : (h + 1) * HD], d_score))
                dk.append(nn(d_score, q))
            dq = jnp.transpose(jnp.concatenate(dq_t, axis=0)).astype(BF16)
            dk = jnp.where(low, dk[0], dk[1]).astype(BF16)
            for n, part in enumerate((dq, dk)):
                dqkv[:, n * C + p * 128 : n * C + (p + 1) * 128] = part
                grads[2 + c, (2 * k + n) * C : (2 * k + n + 1) * C, :] = nn(normed_t[...], part)
            if k == 0:
                hook()

    def span(start, n):
        return pl.ds(pl.multiple_of(start, 8), n)

    core = me["seq_2"]
    half_rows = CHUNK // 2
    COLORS = (("seq_0", "seq_1"), ("seq_1", "seq_0"))

    def place(color, level):
        first, second = COLORS[color]
        at = core * half_rows + color * 512
        if level > 0:
            at = at + me[first] * 128
        if level > 1:
            at = at + me[second] * 32
        return at

    def r_wait_recv(ref, stage, p):
        remote(ref, ref, r_send.at[stage, p], r_recv.at[stage, p], here).wait_recv()

    def r_wait_send(ref, stage, p):
        remote(ref, ref, r_send.at[stage, p], r_recv.at[stage, p], here).wait_send()

    def r_start(src, dst, stage, p, axis, t):
        remote(src, dst, r_send.at[stage, p], r_recv.at[stage, p], {axis: t}).start()

    def s_core(p):
        r_start(grads.at[p, span((1 - core) * half_rows, half_rows)], core_buf.at[p], 0, p, "seq_2", 1 - core)

    def s_first(p):
        r_wait_recv(core_buf.at[p], 0, p)
        acc[p] = grads[p, span(core * half_rows, half_rows), :] + core_buf[p]
        for d in range(3):
            for color, (first, _) in enumerate(COLORS):
                t = peers(first)[d]
                r_start(acc.at[p, span(color * 512 + t * 128, 128)], first_buf.at[p, color, d], 1, p, first, t)

    def s_second(p):
        r_wait_recv(first_buf.at[p], 1, p)
        for color, (first, _) in enumerate(COLORS):
            got = first_buf[p, color, 0] + first_buf[p, color, 1] + first_buf[p, color, 2]
            acc2[p, color * 128 : (color + 1) * 128, :] = acc[p, span(color * 512 + me[first] * 128, 128), :] + got
        for d in range(3):
            for color, (_, second) in enumerate(COLORS):
                t = peers(second)[d]
                r_start(acc2.at[p, span(color * 128 + t * 32, 32)], second_buf.at[p, color, d], 2, p, second, t)

    def s_z(p):
        r_wait_recv(second_buf.at[p], 2, p)
        for color, (_, second) in enumerate(COLORS):
            got = second_buf[p, color, 0] + second_buf[p, color, 1] + second_buf[p, color, 2]
            acc3[p, color * 32 : (color + 1) * 32, :] = acc2[p, span(color * 128 + me[second] * 32, 32), :] + got
        for d, t in enumerate(peers("dp")):
            r_start(acc3.at[p, span(t * 8, 8)], z_buf.at[p, d], 3, p, "dp", t)

    z = me["dp"]
    z_color, z_block = z // 4, lax.rem(z, 4)
    z_place = (1 - z_color) * place(0, 2) + z_color * place(1, 2) + z_block * 8

    def s_gather_z(p):
        r_wait_recv(z_buf.at[p], 3, p)
        total = acc3[p, span(z * 8, 8), :]
        for d in range(7):
            total = total + z_buf[p, d]
        own = span(z_place, 8)
        res[p, own, :] = total.astype(BF16)
        for t in peers("dp"):
            r_start(res.at[p, own], res.at[p, own], 4, p, "dp", t)

    def s_gather_second(p):
        r_wait_recv(res.at[p, pl.ds(0, 56)], 4, p)
        for d in range(3):
            for color, (_, second) in enumerate(COLORS):
                own = span(place(color, 2), 32)
                r_start(res.at[p, own], res.at[p, own], 5, p, second, peers(second)[d])

    def s_gather_first(p):
        r_wait_recv(res.at[p, pl.ds(0, 192)], 5, p)
        for d in range(3):
            for color, (first, _) in enumerate(COLORS):
                own = span(place(color, 1), 128)
                r_start(res.at[p, own], res.at[p, own], 6, p, first, peers(first)[d])

    def s_gather_core(p):
        r_wait_recv(res.at[p, pl.ds(0, 768)], 6, p)
        own = span(core * half_rows, half_rows)
        r_start(res.at[p, own], res.at[p, own], 7, p, "seq_2", 1 - core)

    def finish(p):
        r_wait_recv(res.at[p, pl.ds(0, half_rows)], 7, p)

    def gain_stage(k, axis, buf, value):
        m = me[axis]
        buf[m] = value
        for t in peers(axis):
            remote(buf.at[m], buf.at[m], g_send.at[k], g_recv.at[k], {axis: t}).start()

    def gain_sum(k, axis, buf):
        n = AXES[axis]
        ref = buf.at[pl.ds(0, n - 1)]
        copy = remote(ref, ref, g_send.at[k], g_recv.at[k], here)
        copy.wait_recv()
        copy.wait_send()
        total = buf[0]
        for j in range(1, n):
            total = total + buf[j]
        return total

    values_part(0, lambda: None)
    s_core(0)
    values_part(1, lambda: s_first(0))
    s_core(1)
    keys_part(0, lambda: s_first(1))
    s_core(2)
    keys_part(1, lambda: s_first(2))
    s_core(3)

    d_normed = nt(dqkv[...], wqkv_ref[...])
    s_first(3)
    standard = xhat[...]
    gg = jnp.sum(d_normed * standard, axis=0, keepdims=True)
    for j in range(8):
        gg_ref[j : j + 1, :] = gg[:, j * 128 : (j + 1) * 128] if j < 4 else jnp.zeros((1, 128), F32)
    gain_stage(0, "seq_2", g_core, gg_ref[...])
    scaled = d_normed * gain_ref[...]
    first = jnp.mean(scaled, axis=1, keepdims=True)
    second = jnp.mean(scaled * standard, axis=1, keepdims=True)
    dx = (sgrad[...].astype(F32) + invs[:, 0:1] * (scaled - first - standard * second)).astype(BF16)
    wait_send(send_a.at[others], 0)
    send_a[...] = nn(onehot_ut[...], dx).astype(BF16)
    back[0:CAP, :] = send_a[0:CAP, :]
    gain_stage(1, "seq_0", g_x, gain_sum(0, "seq_2", g_core))
    for p in range(PAIRS):
        s_second(p)
    for p in range(PAIRS):
        s_z(p)
    send_all(send_a, back, 3, -1, FAR_FIRST[0:12])
    gain_stage(2, "seq_1", g_y, gain_sum(1, "seq_0", g_x))
    for p in range(PAIRS):
        s_gather_z(p)
    send_all(send_a, back, 3, -1, FAR_FIRST[12:23])
    for p in range(PAIRS):
        s_gather_second(p)
    gain_stage(3, "dp", g_z, gain_sum(2, "seq_1", g_y))
    for p in range(PAIRS):
        s_gather_first(p)
    send_all(send_a, back, 3, -1, FAR_FIRST[23:31])
    for p in range(PAIRS):
        s_gather_core(p)
    wait_recv(back.at[others], 3)
    out_ref[...] = nn(onehot_pt[...], back[...]).astype(BF16)
    gg_ref[...] = gain_sum(3, "dp", g_z)
    for p in range(PAIRS):
        finish(p)
    wait_send(pos_recv.at[pl.ds(1, N_SEQ - 1)], 2)
    wait_send(send_b.at[others], 1)
    wait_send(send_a.at[others], 3)
    sent = (half_rows, 768, 192, 56, 56, 192, 768, half_rows)
    for p in range(PAIRS):
        for stage in range(8):
            r_wait_send((grads if stage < 4 else res).at[p, pl.ds(0, sent[stage])], stage, p)


def vmem(shape, dtype=F32):
    return pltpu.VMEM(shape, dtype)


DMA = pltpu.SemaphoreType.DMA
VSPEC = pl.BlockSpec(memory_space=pltpu.VMEM)
HBM = pl.BlockSpec(memory_space=pltpu.HBM)


def widen_kernel(res_ref, rows_ref, gg_ref, pts_out, qkv_out, proj_out, gain_out, wide, wide_p, sem):
    copies = [pltpu.make_async_copy(rows_ref, pts_out.at[0], sem.at[0])]
    copies[0].start()
    for r in range(4):
        at = slice(r * 128, (r + 1) * 128)
        for p in range(PAIRS):
            lanes = slice(p * 128, (p + 1) * 128)
            c, k = p // 2, p % 2
            for n, (chunk, row) in enumerate(((2 + c, 2 * k), (2 + c, 2 * k + 1), (c, k))):
                start = row * C + r * 128
                wide[at, n * C + p * 128 : n * C + (p + 1) * 128] = res_ref[chunk, start : start + 128, :].astype(F32)
            start = (2 + r % 2) * C + p * 128
            wide_p[at, lanes] = res_ref[r // 2, start : start + 128, :].astype(F32)
        rows = pl.ds(r * 128, 128)
        copies.append(pltpu.make_async_copy(wide.at[rows], qkv_out.at[rows], sem.at[1 + r]))
        copies.append(pltpu.make_async_copy(wide_p.at[rows], proj_out.at[rows], sem.at[5 + r]))
        copies[-2].start()
        copies[-1].start()
    for j in range(4):
        gain_out[:, j * 128 : (j + 1) * 128] = gg_ref[j : j + 1, :]
    for copy in copies:
        copy.wait()


def per_device(points, cotangent, dest, w_qkv, w_proj, gain):
    big = lambda: vmem((SLOTS, C), BF16)
    grad_local, res, gg = pl.pallas_call(
        block_kernel,
        name="block",
        out_shape=(
            vmem((ROWS, C), BF16),
            vmem((PAIRS, CHUNK, 128), BF16),
            vmem((8, 128)),
        ),
        in_specs=[VSPEC, HBM, HBM, HBM, HBM, VSPEC],
        out_specs=(VSPEC,) * 3,
        scratch_shapes=[
            big(), big(), big(), big(), big(),
            vmem((N_SEQ, 1, 128)), vmem((N_SEQ, 1, 128)), vmem((N_SEQ, 128)),
            vmem((ROWS, 3 * C), BF16), vmem((ROWS, C), BF16), vmem((ROWS, C), BF16),
            vmem((ROWS, C)), vmem((ROWS, 128)), vmem((C, ROWS), BF16), vmem((ROWS, 3 * C), BF16),
            vmem((C, ROWS), BF16), vmem((HEADS, ROWS, ROWS)),
            vmem((ROWS, SLOTS), BF16), vmem((SLOTS, ROWS), BF16), vmem((ROWS, SLOTS), BF16),
            vmem((PAIRS, CHUNK, 128)), vmem((PAIRS, CHUNK // 2, 128)),
            vmem((PAIRS, 256, 128)), vmem((PAIRS, 64, 128)), vmem((PAIRS, CHUNK // 2, 128)),
            vmem((PAIRS, 2, 3, 128, 128)), vmem((PAIRS, 2, 3, 32, 128)), vmem((PAIRS, 7, 8, 128)),
            vmem((2, 8, 128)), vmem((4, 8, 128)), vmem((4, 8, 128)), vmem((8, 8, 128)),
            vmem((ROWS, C), BF16), vmem((ROWS, C), BF16), vmem((C, 3 * C), BF16), vmem((C, C), BF16),
            DMA((4,)), DMA((4,)), DMA((8, PAIRS)), DMA((8, PAIRS)), DMA((4,)), DMA((4,)), DMA((4,)),
        ],
        compiler_params=pltpu.CompilerParams(
            collective_id=0, has_side_effects=True, vmem_limit_bytes=56 * 2**20
        ),
    )(dest, points[0], cotangent[0], w_qkv, w_proj, gain[None, :])
    grad_points, grad_qkv, grad_proj, gain_gradient = pl.pallas_call(
        widen_kernel,
        name="widen",
        out_shape=(
            jax.ShapeDtypeStruct((1, ROWS, C), BF16),
            jax.ShapeDtypeStruct((C, 3 * C), F32),
            jax.ShapeDtypeStruct((C, C), F32),
            jax.ShapeDtypeStruct((1, C), F32),
        ),
        in_specs=[VSPEC] * 3,
        out_specs=(HBM, HBM, HBM, VSPEC),
        scratch_shapes=[vmem((C, 3 * C)), vmem((C, C)), DMA((9,))],
        compiler_params=pltpu.CompilerParams(vmem_limit_bytes=16 * 2**20),
    )(res, grad_local, gg)
    return (grad_points, grad_qkv, grad_proj, gain_gradient.reshape(C))


def solution(mesh):
    finer = Mesh(mesh.devices.reshape(4, 4, 2, mesh.shape["dp"]), ("seq_0", "seq_1", "seq_2", "dp"))
    placed = (P("dp", SEQ, None), P("dp", SEQ, None), P("dp", SEQ), P(), P(), P())
    return jax.shard_map(
        per_device,
        mesh=finer,
        in_specs=placed,
        out_specs=(P("dp", SEQ, None), P(), P(), P()),
        check_vma=False,
    )
```
